32 devices in a mesh: ctx: 8 (over z, x), head: 4 (over y, core).
Axes of the slice: x: 2, y: 2, z: 4, core: 2. Of those that a mesh axis runs over, the one named last changes fastest.
Arguments:
- keys: bfloat16 [16384, 5120], P('ctx', 'head'), may hold values from -6 to 6
- values: bfloat16 [16384, 5120], P('ctx', 'head'), may hold values from -6 to 6
- queries: bfloat16 [16384, 5120], P('ctx', 'head'), may hold values from -6 to 6
- rates: float32 [16384, 16], P('ctx', 'head'), may hold values from 9.765625e-05 to 0.0009765625
- w_gate: bfloat16 [320, 16, 320], P('ctx', 'head'), may hold values from -0.3125 to 0.3125
- w_up: bfloat16 [320, 16, 320], P('ctx', 'head'), may hold values from -0.3125 to 0.3125
- w_down: bfloat16 [320, 16, 320], P('ctx', 'head'), may hold values from -0.3125 to 0.3125
- gain: float32 [5120], P('head'), may hold values from 0.5 to 1.5
Outputs:
- output: bfloat16 [16384, 5120], P('ctx', 'head')
- new_gate: bfloat16 [320, 16, 320], P('ctx', 'head')
- new_up: bfloat16 [320, 16, 320], P('ctx', 'head')
- new_down: bfloat16 [320, 16, 320], P('ctx', 'head')
The draws below stay inside these ranges and needn't reach their ends.
All inputs are finite; a program needn't handle non-finite values.
Results may differ from the reference program's by a relative error of at most 0.0092.
Values may be sent and summed in bfloat16 or wider, within the bound.
A program may use at most 128 MiB of HBM per device.

```python
import math
import jax
import jax.numpy as jnp
from jax import lax

HEADS = 16
DH = 320
FF = 320
TOKENS = 16384
WIDTH = 5120


def block_scale(own_key, extent, split, smallest, high):
    level, own = 1.0, jax.random.fold_in(own_key, 6)
    for position, parts in split:
        heights = jnp.exp(jax.random.uniform(jax.random.fold_in(own, position), (parts,), jnp.float32, smallest / len(split), high / len(split)))
        level = level * jnp.repeat(heights, extent[position] // parts).reshape([-1 if axis == position else 1 for axis in range(len(extent))])
    return level


def bell_draw(own_key, shape, spread, most, pieces=(), dtype=jnp.bfloat16):
    drawn = spread * jax.random.normal(own_key, shape, jnp.float32)
    if pieces:
        drawn = drawn * block_scale(own_key, shape, pieces, -0.22, 0.18)
    return jnp.clip(drawn, -most, most).astype(dtype)


def setup_inputs(seed: int = 0) -> dict:
    arg_keys = jax.random.split(jax.random.key(seed), 9)
    return {
        "keys": bell_draw(arg_keys[0], (TOKENS, WIDTH), 1.0, 6.0, ((0, 8), (1, 4))),
        "values": bell_draw(arg_keys[1], (TOKENS, WIDTH), 1.0, 6.0, ((0, 8), (1, 4))),
        "queries": bell_draw(arg_keys[2], (TOKENS, WIDTH), 1.0, 6.0, ((0, 8), (1, 4))),
        "rates": jnp.clip(jnp.exp(math.log(0.0009765625) - 2.3025851 * jax.random.uniform(arg_keys[3], (TOKENS, HEADS), jnp.float32) ** block_scale(arg_keys[3], (TOKENS, HEADS), ((0, 8), (1, 4)), -0.2, 0.2)), 9.765625145519152e-05, 0.0009765625),
        "w_gate": bell_draw(arg_keys[4], (FF, HEADS, DH), DH ** -0.5, 0.3125, ((0, 8), (1, 4))),
        "w_up": bell_draw(arg_keys[5], (FF, HEADS, DH), DH ** -0.5, 0.3125, ((0, 8), (1, 4))),
        "w_down": bell_draw(arg_keys[6], (FF, HEADS, DH), FF ** -0.5, 0.3125, ((0, 8), (1, 4))),
        "gain": jnp.clip(1.0 + 0.1 * jax.random.normal(arg_keys[7], (WIDTH,), jnp.float32), 0.5, 1.5),
    }


EPS = 1e-06

def renorm(weight, grad):
    old = weight.astype(jnp.float32)
    updated = old + grad
    old_sq = lax.optimization_barrier(jnp.sum(old * old, axis=0))
    new_sq = lax.optimization_barrier(jnp.sum(updated * updated, axis=0))
    return (updated * (jnp.sqrt(old_sq) * lax.rsqrt(new_sq + EPS))[None, :]).astype(jnp.bfloat16)

def update_head(operands):
    keyh, valueh, rateh, wgate, wup, wdown = operands
    gpre = jnp.dot(keyh, wgate.T, preferred_element_type=jnp.float32)
    upre = jnp.dot(keyh, wup.T, preferred_element_type=jnp.float32)
    sig = jax.nn.sigmoid(gpre)
    act = gpre * sig
    slope = sig * (1.0 + gpre * (1.0 - sig))
    hidden = (act * upre).astype(jnp.bfloat16)
    scaled = (valueh.astype(jnp.float32) * rateh[:, None]).astype(jnp.bfloat16)
    back = jnp.dot(scaled, wdown.T, preferred_element_type=jnp.float32)
    dgate = (back * upre * slope).astype(jnp.bfloat16)
    dup = (back * act).astype(jnp.bfloat16)
    grad_gate = jnp.dot(dgate.T, keyh, preferred_element_type=jnp.float32)
    grad_up = jnp.dot(dup.T, keyh, preferred_element_type=jnp.float32)
    grad_down = jnp.dot(hidden.T, scaled, preferred_element_type=jnp.float32)
    return (renorm(wgate, grad_gate), renorm(wup, grad_up), renorm(wdown, grad_down))

def apply_head(queryh, wgate, wup, wdown):
    gpre = jnp.dot(queryh, wgate.T, preferred_element_type=jnp.float32)
    upre = jnp.dot(queryh, wup.T, preferred_element_type=jnp.float32)
    mixed = (jax.nn.silu(gpre) * upre).astype(jnp.bfloat16)
    return jnp.dot(mixed, wdown, preferred_element_type=jnp.float32)

def reference(keys, values, queries, rates, w_gate, w_up, w_down, gain):
    rows = keys.shape[0]
    keyh = keys.reshape(rows, HEADS, DH).transpose(1, 0, 2)
    valueh = values.reshape(rows, HEADS, DH).transpose(1, 0, 2)
    queryh = queries.reshape(rows, HEADS, DH).transpose(1, 0, 2)
    rateh = rates.T
    new_gate, new_up, new_down = lax.map(update_head, (keyh, valueh, rateh, w_gate.transpose(1, 0, 2), w_up.transpose(1, 0, 2), w_down.transpose(1, 0, 2)))

    def head_squares(operands):
        outh = apply_head(*operands)
        return lax.optimization_barrier(jnp.sum(outh * outh, axis=1))
    squares = lax.optimization_barrier(jnp.sum(lax.map(head_squares, (queryh, new_gate, new_up, new_down)), axis=0))
    scale = lax.rsqrt(squares / (HEADS * DH) + EPS)
    gainh = gain.reshape(HEADS, DH)

    def head_output(operands):
        queryone, wgate, wup, wdown, gainone = operands
        outh = apply_head(queryone, wgate, wup, wdown)
        return (outh * scale[:, None] * gainone[None, :]).astype(jnp.bfloat16)
    output = lax.map(head_output, (queryh, new_gate, new_up, new_down, gainh))
    output = output.transpose(1, 0, 2).reshape(rows, HEADS * DH)
    return (output, new_gate.transpose(1, 0, 2), new_up.transpose(1, 0, 2), new_down.transpose(1, 0, 2))
```

```python
import functools
import math

import jax
import jax.numpy as jnp
from jax import lax
from jax.experimental import pallas as pl
from jax.experimental.pallas import tpu as pltpu
from jax.sharding import PartitionSpec as P

EPS = 1e-06


def inner_size(n):
    inner = 1
    while inner * inner * 4 <= n and n % (inner * 2) == 0:
        inner *= 2
    return inner if inner > 1 or n % 2 else 2


def place(n, inner):
    me = lax.axis_index("ctx")
    return me, me // inner, lax.rem(me, inner), n // inner


def greet(z, x, outer, inner):
    barrier = pltpu.get_barrier_semaphore()
    for s in range(1, outer):
        pl.semaphore_signal(barrier, inc=1, device_id={"ctx": lax.rem(z + s, outer) * inner + x})
    for t in range(1, inner):
        pl.semaphore_signal(barrier, inc=1, device_id={"ctx": z * inner + lax.rem(x + t, inner)})
    pl.semaphore_wait(barrier, outer + inner - 2)


def spread(z, x, outer, inner, own_ref, out_ref, send_sem, recv_sem):
    me = z * inner + x
    copies = {}

    def send(src, block, device, s, t):
        copy = pltpu.make_async_remote_copy(
            src_ref=src,
            dst_ref=out_ref.at[block],
            send_sem=send_sem.at[s, t],
            recv_sem=recv_sem.at[s, t],
            device_id={"ctx": device},
        )
        copy.start()
        copies[s, t] = copy

    for s in range(1, outer):
        send(own_ref, me, lax.rem(z + s, outer) * inner + x, s, 0)
    for t in range(1, inner):
        send(own_ref, me, z * inner + lax.rem(x + t, inner), 0, t)
    for s in range(1, outer):
        copies[s, 0].wait_recv()
        block = lax.rem(z + outer - s, outer) * inner + x
        for t in range(1, inner):
            send(out_ref.at[block], block, z * inner + lax.rem(x + t, inner), s, t)
    for (s, t), copy in copies.items():
        if t:
            copy.wait_recv()
    for copy in copies.values():
        copy.wait_send()


def gather_kernel(n, inner, own_ref, out_ref, local_sem, send_sem, recv_sem):
    me, z, x, outer = place(n, inner)
    greet(z, x, outer, inner)
    keep = pltpu.make_async_copy(own_ref, out_ref.at[me], local_sem)
    keep.start()
    spread(z, x, outer, inner, own_ref, out_ref, send_sem, recv_sem)
    keep.wait()


def update_kernel(
    n, inner, grad_ref, old_ref, out_ref, near, part, far, fresh,
    local_sem, near_send, near_recv, far_send, far_recv, send_sem, recv_sem,
):
    me, z, x, outer = place(n, inner)
    greet(z, x, outer, inner)
    order = list(range(1, outer)) + [0]
    first = {}
    for s in order:
        row = lax.rem(z + s, outer) * inner
        for t in range(1, inner):
            column = lax.rem(x + t, inner)
            copy = pltpu.make_async_remote_copy(
                src_ref=grad_ref.at[row + column],
                dst_ref=near.at[s, t - 1],
                send_sem=near_send.at[s, t],
                recv_sem=near_recv.at[s, t],
                device_id={"ctx": z * inner + column},
            )
            copy.start()
            first[s, t] = copy
    second = {}
    total = None
    for s in order:
        row = lax.rem(z + s, outer) * inner
        total = grad_ref[row + x].astype(jnp.float32)
        for t in range(1, inner):
            first[s, t].wait_recv()
            total = total + near[s, t - 1].astype(jnp.float32)
        if s:
            part[s] = total.astype(part.dtype)
            copy = pltpu.make_async_remote_copy(
                src_ref=part.at[s],
                dst_ref=far.at[s],
                send_sem=far_send.at[s],
                recv_sem=far_recv.at[s],
                device_id={"ctx": row + x},
            )
            copy.start()
            second[s] = copy
    for s, copy in second.items():
        copy.wait_recv()
        total = total + far[s].astype(jnp.float32)
    old = old_ref[...].astype(jnp.float32)
    updated = old + total
    old_sq = jnp.sum(old * old, axis=1, keepdims=True)
    new_sq = jnp.sum(updated * updated, axis=1, keepdims=True)
    fresh[...] = (updated * (jnp.sqrt(old_sq) * lax.rsqrt(new_sq + EPS))).astype(fresh.dtype)
    keep = pltpu.make_async_copy(fresh, out_ref.at[me], local_sem)
    keep.start()
    keep.wait()
    spread(z, x, outer, inner, out_ref.at[me], out_ref, send_sem, recv_sem)
    for copy in first.values():
        copy.wait_send()
    for copy in second.values():
        copy.wait_send()


def vmem(count):
    return [pl.BlockSpec(memory_space=pltpu.VMEM)] * count


def gather(own, n):
    inner = inner_size(n)
    outer = n // inner
    return pl.pallas_call(
        functools.partial(gather_kernel, n, inner),
        out_shape=jax.ShapeDtypeStruct((n,) + own.shape, own.dtype),
        in_specs=vmem(1),
        out_specs=vmem(1)[0],
        scratch_shapes=[pltpu.SemaphoreType.DMA]
        + [pltpu.SemaphoreType.DMA((outer, inner))] * 2,
        compiler_params=pltpu.CompilerParams(collective_id=0, has_side_effects=True),
        name="gather_weights",
    )(own)


def update(grads, old, n):
    inner = inner_size(n)
    outer = n // inner
    block = grads.shape[1:]
    return pl.pallas_call(
        functools.partial(update_kernel, n, inner),
        out_shape=jax.ShapeDtypeStruct(grads.shape, grads.dtype),
        in_specs=vmem(2),
        out_specs=vmem(1)[0],
        scratch_shapes=[
            pltpu.VMEM((outer, max(inner - 1, 1)) + block, grads.dtype),
            pltpu.VMEM((outer,) + block, grads.dtype),
            pltpu.VMEM((outer,) + block, grads.dtype),
            pltpu.VMEM(block, grads.dtype),
            pltpu.SemaphoreType.DMA,
        ]
        + [pltpu.SemaphoreType.DMA((outer, inner))] * 2
        + [pltpu.SemaphoreType.DMA((outer,))] * 2
        + [pltpu.SemaphoreType.DMA((outer, inner))] * 2,
        compiler_params=pltpu.CompilerParams(collective_id=1, has_side_effects=True),
        name="update_weights",
    )(grads, old)


def dot(a, b, left, right):
    return lax.dot_general(a, b, (((left,), (right,)), ((), ())), preferred_element_type=jnp.float32)


def grads_kernel(key_ref, value_ref, rate_ref, weight_ref, out_ref, acc):
    step = pl.program_id(0)

    @pl.when(step == 0)
    def _():
        acc[...] = jnp.zeros_like(acc)

    heads, width = weight_ref.shape[1:3]
    for h in range(heads):
        columns = slice(h * width, (h + 1) * width)
        key = key_ref[:, columns]
        gpre = dot(key, weight_ref[0, h], 1, 0)
        upre = dot(key, weight_ref[1, h], 1, 0)
        scaled = (value_ref[:, columns].astype(jnp.float32) * rate_ref[:, h : h + 1]).astype(jnp.bfloat16)
        back = dot(scaled, weight_ref[2, h], 1, 0)
        sig = jax.nn.sigmoid(gpre)
        act = gpre * sig
        slope = sig * (1.0 + gpre * (1.0 - sig))
        acc[0, h] += dot(key, (back * upre * slope).astype(jnp.bfloat16), 0, 0)
        acc[1, h] += dot(key, (back * act).astype(jnp.bfloat16), 0, 0)
        acc[2, h] += dot(scaled, (act * upre).astype(jnp.bfloat16), 0, 0)

    @pl.when(step == pl.num_programs(0) - 1)
    def _():
        out_ref[...] = acc[...].astype(out_ref.dtype)


def apply_kernel(query_ref, weight_ref, out_ref, square_ref):
    heads, width = weight_ref.shape[1:3]
    squares = None
    for h in range(heads):
        columns = slice(h * width, (h + 1) * width)
        query = query_ref[:, columns]
        gate = dot(query, weight_ref[0, h], 1, 0)
        up = dot(query, weight_ref[1, h], 1, 0)
        mixed = (jax.nn.silu(gate) * up).astype(jnp.bfloat16)
        out = dot(mixed, weight_ref[2, h], 1, 1)
        part = jnp.sum(out * out, axis=1, keepdims=True)
        squares = part if squares is None else squares + part
        out_ref[:, columns] = out.astype(out_ref.dtype)
    square_ref[...] = squares


def tile(rows, width):
    return pl.BlockSpec((rows, width), lambda i: (i, 0))


def fixed(shape):
    return pl.BlockSpec(shape, lambda i: (0,) * len(shape))


def token_grads(keys, values, rates, weights):
    rows, width = keys.shape
    step = math.gcd(rows, 512)
    return pl.pallas_call(
        grads_kernel,
        grid=(rows // step,),
        out_shape=jax.ShapeDtypeStruct(weights.shape, jnp.bfloat16),
        in_specs=[tile(step, width), tile(step, width), tile(step, rates.shape[1]), fixed(weights.shape)],
        out_specs=fixed(weights.shape),
        scratch_shapes=[pltpu.VMEM(weights.shape, jnp.float32)],
        name="token_grads",
    )(keys, values, rates, weights)


def apply(queries, weights):
    rows, width = queries.shape
    step = math.gcd(rows, 512)
    return pl.pallas_call(
        apply_kernel,
        grid=(rows // step,),
        out_shape=(
            jax.ShapeDtypeStruct((rows, width), jnp.bfloat16),
            jax.ShapeDtypeStruct((rows, 1), jnp.float32),
        ),
        in_specs=[tile(step, width), fixed(weights.shape)],
        out_specs=(tile(step, width), tile(step, 1)),
        name="apply_weights",
    )(queries, weights)


def per_device(n, width_all, keys, values, queries, rates, w_gate, w_up, w_down, gain):
    rows = keys.shape[0]
    units, heads, width = w_gate.shape
    f32 = jnp.float32
    own = jnp.stack([w_gate, w_up, w_down]).transpose(0, 2, 1, 3)
    own = own.reshape(3 * heads, units, width)
    full = gather(own, n).transpose(1, 3, 0, 2)
    full = full.reshape(3, heads, width, n * units)
    grads = token_grads(keys, values, rates, full)
    block = (n, 3 * heads * width // n, n * units)
    old = lax.dynamic_index_in_dim(full.reshape(block), lax.axis_index("ctx"), 0, keepdims=False)
    fresh = update(grads.reshape(block), old, n).reshape(full.shape)
    mine = lax.dynamic_slice_in_dim(fresh, lax.axis_index("ctx") * units, units, 3)
    mine = mine.transpose(0, 3, 1, 2)
    outs, squares = apply(queries, fresh)
    squares = lax.psum(squares.reshape(rows), "head")
    scale = lax.rsqrt(squares / width_all + EPS)
    output = (outs.astype(f32) * scale[:, None] * gain[None]).astype(jnp.bfloat16)
    return (output, mine[0], mine[1], mine[2])


def solution(mesh):
    weight = P("ctx", "head", None)
    token = P("ctx", "head")

    def whole(keys, *rest):
        body = functools.partial(per_device, mesh.shape["ctx"], keys.shape[1])
        return jax.shard_map(
            body,
            mesh=mesh,
            in_specs=(token,) * 4 + (weight,) * 3 + (P("head"),),
            out_specs=(token, weight, weight, weight),
            check_vma=False,
        )(keys, *rest)

    return whole
```

```python
import functools
import math

import jax
import jax.numpy as jnp
from jax import lax
from jax.experimental import pallas as pl
from jax.experimental.pallas import tpu as pltpu
from jax.sharding import PartitionSpec as P

EPS = 1e-06


def inner_size(n):
    inner = 1
    while inner * inner * 4 <= n and n % (inner * 2) == 0:
        inner *= 2
    return inner if inner > 1 or n % 2 else 2


def place(n, inner):
    me = lax.axis_index("ctx")
    return me, me // inner, lax.rem(me, inner), n // inner


def greet(z, x, outer, inner):
    barrier = pltpu.get_barrier_semaphore()
    for s in range(1, outer):
        pl.semaphore_signal(barrier, inc=1, device_id={"ctx": lax.rem(z + s, outer) * inner + x})
    for t in range(1, inner):
        pl.semaphore_signal(barrier, inc=1, device_id={"ctx": z * inner + lax.rem(x + t, inner)})
    pl.semaphore_wait(barrier, outer + inner - 2)


def spread(z, x, outer, inner, own_ref, out_ref, send_sem, recv_sem):
    me = z * inner + x
    copies = {}

    def send(src, block, device, s, t):
        copy = pltpu.make_async_remote_copy(
            src_ref=src,
            dst_ref=out_ref.at[block],
            send_sem=send_sem.at[s, t],
            recv_sem=recv_sem.at[s, t],
            device_id={"ctx": device},
        )
        copy.start()
        copies[s, t] = copy

    for s in range(1, outer):
        send(own_ref, me, lax.rem(z + s, outer) * inner + x, s, 0)
    for t in range(1, inner):
        send(own_ref, me, z * inner + lax.rem(x + t, inner), 0, t)
    for s in range(1, outer):
        copies[s, 0].wait_recv()
        block = lax.rem(z + outer - s, outer) * inner + x
        for t in range(1, inner):
            send(out_ref.at[block], block, z * inner + lax.rem(x + t, inner), s, t)
    for (s, t), copy in copies.items():
        if t:
            copy.wait_recv()
    for copy in copies.values():
        copy.wait_send()


def gather_kernel(n, inner, own_ref, out_ref, local_sem, send_sem, recv_sem):
    me, z, x, outer = place(n, inner)
    greet(z, x, outer, inner)
    keep = pltpu.make_async_copy(own_ref, out_ref.at[me], local_sem)
    keep.start()
    spread(z, x, outer, inner, own_ref, out_ref, send_sem, recv_sem)
    keep.wait()


def update_kernel(
    n, inner, grad_ref, old_ref, out_ref, near, part, far, fresh,
    local_sem, near_send, near_recv, far_send, far_recv, send_sem, recv_sem,
):
    me, z, x, outer = place(n, inner)
    greet(z, x, outer, inner)
    order = list(range(1, outer)) + [0]
    first = {}
    for s in order:
        row = lax.rem(z + s, outer) * inner
        for t in range(1, inner):
            column = lax.rem(x + t, inner)
            copy = pltpu.make_async_remote_copy(
                src_ref=grad_ref.at[row + column],
                dst_ref=near.at[s, t - 1],
                send_sem=near_send.at[s, t],
                recv_sem=near_recv.at[s, t],
                device_id={"ctx": z * inner + column},
            )
            copy.start()
            first[s, t] = copy
    second = {}
    total = None
    for s in order:
        row = lax.rem(z + s, outer) * inner
        total = grad_ref[row + x].astype(jnp.float32)
        for t in range(1, inner):
            first[s, t].wait_recv()
            total = total + near[s, t - 1].astype(jnp.float32)
        if s:
            part[s] = total.astype(part.dtype)
            copy = pltpu.make_async_remote_copy(
                src_ref=part.at[s],
                dst_ref=far.at[s],
                send_sem=far_send.at[s],
                recv_sem=far_recv.at[s],
                device_id={"ctx": row + x},
            )
            copy.start()
            second[s] = copy
    for s, copy in second.items():
        copy.wait_recv()
        total = total + far[s].astype(jnp.float32)
    old = old_ref[me].astype(jnp.float32)
    updated = old + total
    old_sq = jnp.sum(old * old, axis=1, keepdims=True)
    new_sq = jnp.sum(updated * updated, axis=1, keepdims=True)
    fresh[...] = (updated * (jnp.sqrt(old_sq) * lax.rsqrt(new_sq + EPS))).astype(fresh.dtype)
    keep = pltpu.make_async_copy(fresh, out_ref.at[me], local_sem)
    keep.start()
    keep.wait()
    spread(z, x, outer, inner, out_ref.at[me], out_ref, send_sem, recv_sem)
    for copy in first.values():
        copy.wait_send()
    for copy in second.values():
        copy.wait_send()


def vmem(count):
    return [pl.BlockSpec(memory_space=pltpu.VMEM)] * count


def gather(own, n):
    inner = inner_size(n)
    outer = n // inner
    return pl.pallas_call(
        functools.partial(gather_kernel, n, inner),
        out_shape=jax.ShapeDtypeStruct((n,) + own.shape, own.dtype),
        in_specs=vmem(1),
        out_specs=vmem(1)[0],
        scratch_shapes=[pltpu.SemaphoreType.DMA]
        + [pltpu.SemaphoreType.DMA((outer, inner))] * 2,
        compiler_params=pltpu.CompilerParams(collective_id=0, has_side_effects=True),
        name="gather_weights",
    )(own)


def update(grads, old, n):
    inner = inner_size(n)
    outer = n // inner
    block = grads.shape[1:]
    return pl.pallas_call(
        functools.partial(update_kernel, n, inner),
        out_shape=jax.ShapeDtypeStruct(grads.shape, grads.dtype),
        in_specs=vmem(2),
        out_specs=vmem(1)[0],
        scratch_shapes=[
            pltpu.VMEM((outer, max(inner - 1, 1)) + block, grads.dtype),
            pltpu.VMEM((outer,) + block, grads.dtype),
            pltpu.VMEM((outer,) + block, grads.dtype),
            pltpu.VMEM(block, grads.dtype),
            pltpu.SemaphoreType.DMA,
        ]
        + [pltpu.SemaphoreType.DMA((outer, inner))] * 2
        + [pltpu.SemaphoreType.DMA((outer,))] * 2
        + [pltpu.SemaphoreType.DMA((outer, inner))] * 2,
        compiler_params=pltpu.CompilerParams(collective_id=1, has_side_effects=True),
        name="update_weights",
    )(grads, old)


def dot(a, b, left, right):
    return lax.dot_general(a, b, (((left,), (right,)), ((), ())), preferred_element_type=jnp.float32)


def grads_kernel(key_ref, value_ref, rate_ref, weight_ref, out_ref, acc):
    step = pl.program_id(0)

    @pl.when(step == 0)
    def _():
        acc[...] = jnp.zeros_like(acc)

    heads, width = weight_ref.shape[1:3]
    for h in range(heads):
        columns = slice(h * width, (h + 1) * width)
        key = key_ref[:, columns]
        gpre = dot(key, weight_ref[0, h], 1, 0)
        upre = dot(key, weight_ref[1, h], 1, 0)
        scaled = (value_ref[:, columns].astype(jnp.float32) * rate_ref[:, h : h + 1]).astype(jnp.bfloat16)
        back = dot(scaled, weight_ref[2, h], 1, 0)
        sig = jax.nn.sigmoid(gpre)
        act = gpre * sig
        slope = sig * (1.0 + gpre * (1.0 - sig))
        acc[0, h] += dot(key, (back * upre * slope).astype(jnp.bfloat16), 0, 0)
        acc[1, h] += dot(key, (back * act).astype(jnp.bfloat16), 0, 0)
        acc[2, h] += dot(scaled, (act * upre).astype(jnp.bfloat16), 0, 0)

    @pl.when(step == pl.num_programs(0) - 1)
    def _():
        out_ref[...] = acc[...].astype(out_ref.dtype)


def apply_kernel(query_ref, weight_ref, out_ref, square_ref):
    heads, width = weight_ref.shape[1:3]
    squares = None
    for h in range(heads):
        columns = slice(h * width, (h + 1) * width)
        query = query_ref[:, columns]
        gate = dot(query, weight_ref[0, h], 1, 0)
        up = dot(query, weight_ref[1, h], 1, 0)
        mixed = (jax.nn.silu(gate) * up).astype(jnp.bfloat16)
        out = dot(mixed, weight_ref[2, h], 1, 1)
        part = jnp.sum(out * out, axis=1, keepdims=True)
        squares = part if squares is None else squares + part
        out_ref[:, columns] = out.astype(out_ref.dtype)
    square_ref[...] = squares


def tile(rows, width):
    return pl.BlockSpec((rows, width), lambda i: (i, 0))


def fixed(shape):
    return pl.BlockSpec(shape, lambda i: (0,) * len(shape))


def token_grads(keys, values, rates, weights):
    rows, width = keys.shape
    step = math.gcd(rows, 512)
    return pl.pallas_call(
        grads_kernel,
        grid=(rows // step,),
        out_shape=jax.ShapeDtypeStruct(weights.shape, jnp.bfloat16),
        in_specs=[tile(step, width), tile(step, width), tile(step, rates.shape[1]), fixed(weights.shape)],
        out_specs=fixed(weights.shape),
        scratch_shapes=[pltpu.VMEM(weights.shape, jnp.float32)],
        name="token_grads",
    )(keys, values, rates, weights)


def apply(queries, weights):
    rows, width = queries.shape
    step = math.gcd(rows, 512)
    return pl.pallas_call(
        apply_kernel,
        grid=(rows // step,),
        out_shape=(
            jax.ShapeDtypeStruct((rows, width), jnp.bfloat16),
            jax.ShapeDtypeStruct((rows, 1), jnp.float32),
        ),
        in_specs=[tile(step, width), fixed(weights.shape)],
        out_specs=(tile(step, width), tile(step, 1)),
        name="apply_weights",
    )(queries, weights)


def per_device(n, width_all, keys, values, queries, rates, w_gate, w_up, w_down, gain):
    rows = keys.shape[0]
    units, heads, width = w_gate.shape
    f32 = jnp.float32
    own = jnp.stack([w_gate, w_up, w_down]).transpose(0, 2, 1, 3)
    own = own.reshape(3 * heads, units, width)
    full = gather(own, n).transpose(1, 3, 0, 2)
    full = full.reshape(3, heads, width, n * units)
    grads = token_grads(keys, values, rates, full)
    block = (n, 3 * heads * width // n, n * units)
    fresh = update(grads.reshape(block), full.reshape(block), n).reshape(full.shape)
    mine = lax.dynamic_slice_in_dim(fresh, lax.axis_index("ctx") * units, units, 3)
    mine = mine.transpose(0, 3, 1, 2)
    outs, squares = apply(queries, fresh)
    squares = lax.psum(squares.reshape(rows), "head")
    scale = lax.rsqrt(squares / width_all + EPS)
    output = (outs.astype(f32) * scale[:, None] * gain[None]).astype(jnp.bfloat16)
    return (output, mine[0], mine[1], mine[2])


def solution(mesh):
    weight = P("ctx", "head", None)
    token = P("ctx", "head")

    def whole(keys, *rest):
        body = functools.partial(per_device, mesh.shape["ctx"], keys.shape[1])
        return jax.shard_map(
            body,
            mesh=mesh,
            in_specs=(token,) * 4 + (weight,) * 3 + (P("head"),),
            out_specs=(token, weight, weight, weight),
            check_vma=False,
        )(keys, *rest)

    return whole
```
